32 devices in a mesh: parts: 2 (over y), node: 4 (over x, core), local: 4 (over z).
Axes of the slice: x: 2, y: 2, z: 4, core: 2. Of those that a mesh axis runs over, the one named last changes fastest.
Arguments:
- tokens: bfloat16 [4096, 3584], P(('parts', 'node', 'local')), parts along dimension 0, may hold values from -6 to 6
- expert_ids: int32 [4096, 3], P(('parts', 'node', 'local')), parts along dimension 0, may hold values from 0 to 15, all different within a row; in each aligned block of 128 rows (0 to 127, 128 to 255, ...) at most 32 rows name the same one
- gate_weights: float32 [4096, 3], P(('parts', 'node', 'local')), parts along dimension 0, may hold values from 0.1 to 1
- gate_proj: bfloat16 [16, 3584, 1024], P(('node', 'local')), may hold values from -0.09375 to 0.09375
- up_proj: bfloat16 [16, 3584, 1024], P(('node', 'local')), may hold values from -0.09375 to 0.09375
- down_proj: bfloat16 [16, 1024, 3584], P(('node', 'local')), may hold values from -0.1875 to 0.1875
Outputs:
- combined: bfloat16 [4096, 3584], P(('parts', 'node', 'local')), parts along dimension 0
The draws below stay inside these ranges and needn't reach their ends.
There are 2 independent parts, one for each index of `parts`. The reference program is written for one: setup_inputs(seed, part) draws one part's arguments, and reference() takes and returns one part's arrays. A program takes and returns all parts, laid end to end along the dimension named above; an argument that names none is the same for every part. Nothing has to cross between parts.
Inputs may be any that keep to these rules, and one draw needn't show every extreme that they name: `expert_ids`: each row names 3 different experts; among the rows of one device no expert is named by more than 32 rows, a bound that some block reaches.
All inputs are finite; a program needn't handle non-finite values.
Results may differ from the reference program's by a relative error of at most 0.0058.
Values may be sent and summed in bfloat16 or wider, within the bound.
No kernel may reach another device: no remote copies, remote signals or barrier semaphores. Data moves between devices by JAX's collectives and lax.ppermute only.
A program may use at most 128 MiB of HBM per device.

```python
import math
import jax
import jax.numpy as jnp
import numpy as np
from jax import lax

D = 3584
FF = 1024
EPG = 4
TOPK = 3
TOK_DEV = 128
EXPERTS = 16
WSPLIT = 1
FF_DEV = 1024
CAP = 32
TOKENS = 2048
N_NODE = 4
N_LOCAL = 4


def level_of(stream_key, shape, cuts, smallest, high):
    def one(dim, blocks):
        steps = jax.random.uniform(jax.random.fold_in(jax.random.fold_in(stream_key, 6), dim), (blocks,), jnp.float32, smallest / len(cuts), high / len(cuts))
        return jnp.repeat(jnp.exp(steps), shape[dim] // blocks).reshape((-1,) + (1,) * (len(shape) - dim - 1))

    loudness = one(*cuts[0])
    for cut in cuts[1:]:
        loudness = loudness * one(*cut)
    return loudness


def routed_block(own_key, own, number, rows, count, top, most, lean):
    order = jax.random.permutation(own_key, count)
    crowded, ordinary = shares(count, rows * top, most, lean, True), shares(count, rows * top, most, lean, False)
    places = jnp.arange(count)

    def named(sizes, rotation):
        used = int((sizes > 0).sum())
        fixed = max(1, used // 4)
        passed = fixed + (places - fixed + rotation * (used - fixed)) % max(1, count - fixed)
        return jnp.zeros((count,), jnp.int32).at[order[jnp.where(places < fixed, places, passed)]].set(jnp.asarray(sizes, jnp.int32))

    sizes = jnp.where(number % 4 == 0, named(crowded, number // 4), named(ordinary, number - number // 4 - 1))
    mixed = jax.random.permutation(jax.random.fold_in(own, 3), count)
    giver, sink = mixed[0:count // 2 * 2:2], mixed[1:count // 2 * 2:2]
    room = jnp.minimum(sizes[giver] - 1, most - sizes[sink]) // 2
    room = jnp.where((giver == order[0]) | (sink == order[0]) | (sizes[sink] == 0), 0, jnp.maximum(room, 0))
    passed = jax.random.randint(jax.random.fold_in(own, 4), (count // 2,), 0, 1 << 20) % (room + 1)
    sizes = sizes.at[giver].add(-passed).at[sink].add(passed)
    members = jnp.searchsorted(jnp.cumsum(sizes), jnp.arange(rows * top), side="right").astype(jnp.int32)
    table = members.reshape(top, rows).T
    table = table[jax.random.permutation(jax.random.fold_in(own, 1), rows)]
    rotation = jax.random.randint(jax.random.fold_in(own, 2), (rows, 1), 0, top)
    return jnp.take_along_axis(table, (jnp.arange(top)[None, :] + rotation) % top, axis=1)


def shares(amount, total, bound, skew, full):
    loads = [(1 << 20) // math.isqrt(grade ** skew) + 1 for grade in range(1, amount + 1)]
    largest = bound if full else min(bound, max(-(-total // amount), total * loads[0] // sum(loads)))
    least = 1 if total - largest >= amount - 1 else 0
    counts, rest = [largest] + [least] * (amount - 1), total - largest - least * (amount - 1)
    while rest > 0:
        free = [i for i in range(1, amount) if counts[i] < largest] or [i for i in range(1, amount) if counts[i] < bound]
        pool, remaining = sum([loads[i] for i in free]), rest
        for i in free:
            addition = min(bound - counts[i], max(1, remaining * loads[i] // pool), rest)
            counts[i] = counts[i] + addition
            rest = rest - addition
    return np.array(counts)


def scatter_about(own_key, shape, deviation, most, shards=(), kind=jnp.bfloat16):
    result = jax.random.normal(own_key, shape, jnp.float32) * deviation
    if len(shards) > 0:
        result = level_of(own_key, shape, shards, -0.22, 0.18) * result
    return jnp.clip(result, min=-most, max=most).astype(kind)


def setup_inputs(seed: int = 0, part: int = 0) -> dict:
    keys = jax.random.split(jax.random.key(seed), 7)
    part_splits = jax.random.split(jax.random.fold_in(keys[6], part), 7)
    tokens = scatter_about(part_splits[0], (TOKENS, D), 1.0, 6.0, ((0, 16),))
    expert_ids_keys = jax.random.split(jax.random.fold_in(part_splits[1], 1), TOKENS // TOK_DEV)
    expert_ids_turns = jax.random.permutation(jax.random.fold_in(part_splits[1], 3), TOKENS // TOK_DEV)
    expert_ids = jax.vmap(lambda own, number: routed_block(jax.random.fold_in(part_splits[1], 2), own, number, TOK_DEV, EXPERTS, TOPK, CAP, 2))(expert_ids_keys, expert_ids_turns).reshape((TOKENS, TOPK))
    gate_weights = jnp.clip(jnp.exp(math.log(1.0) - 2.3025851 * jax.random.uniform(part_splits[2], (TOKENS, TOPK), jnp.float32) ** level_of(part_splits[2], (TOKENS, TOPK), ((0, 16),), -0.2, 0.2)), 0.1, 1.0)
    gate_proj = scatter_about(keys[3], (EXPERTS * WSPLIT, D, FF_DEV), D ** -0.5, 0.09375, ((0, 16),))
    up_proj = scatter_about(keys[4], (EXPERTS * WSPLIT, D, FF_DEV), D ** -0.5, 0.09375, ((0, 16),))
    down_proj = scatter_about(keys[5], (EXPERTS * WSPLIT, FF_DEV, D), FF ** -0.5, 0.1875, ((0, 16),))
    return dict(tokens=tokens, expert_ids=expert_ids, gate_weights=gate_weights, gate_proj=gate_proj, up_proj=up_proj, down_proj=down_proj)


def expert_rows(rows, gate_mat, up_mat, down_mat):
    gate_act = jnp.dot(rows, gate_mat, preferred_element_type=jnp.float32)
    up_act = jnp.dot(rows, up_mat, preferred_element_type=jnp.float32)
    hidden = (jax.nn.silu(gate_act) * up_act).astype(jnp.bfloat16)
    return jnp.dot(hidden, down_mat, preferred_element_type=jnp.float32).astype(jnp.bfloat16)


def reference(tokens, expert_ids, gate_weights, gate_proj, up_proj, down_proj):
    wsplit = N_LOCAL // EPG
    max_rows = N_NODE * N_LOCAL * CAP

    def visit(accumulated, inputs):
        gate_mat, up_mat, down_mat, shard_id = inputs
        expert = (shard_id // wsplit).astype(jnp.int32)
        matched = expert_ids == expert
        weight = jnp.sum(jnp.where(matched, gate_weights, jnp.zeros_like(gate_weights)), axis=1)
        chosen = jnp.any(matched, axis=1)
        positions = jnp.nonzero(chosen, size=max_rows, fill_value=0)[0].astype(jnp.int32)
        live_count = jnp.sum(chosen.astype(jnp.int32))
        is_live = jnp.arange(max_rows, dtype=jnp.int32) < live_count
        row_weight = jnp.where(is_live, weight[positions], jnp.zeros_like(weight[positions]))
        partial_value = expert_rows(tokens[positions], gate_mat, up_mat, down_mat)
        accumulated = accumulated.at[positions].add(partial_value.astype(jnp.float32) * row_weight[:, None])
        return accumulated, None

    shard_ids = jnp.arange(N_NODE * N_LOCAL, dtype=jnp.int32)
    start = jnp.zeros((TOKENS, D), jnp.float32)
    accumulated, unused = lax.scan(visit, start, (gate_proj, up_proj, down_proj, shard_ids))
    return accumulated.astype(jnp.bfloat16)
```

```python
import jax
import jax.numpy as jnp
from jax import lax
from jax.sharding import PartitionSpec as P

EPG = 4
IN_CHUNKS = 1
OUT_CHUNKS = 1


def on_device(tokens, expert_ids, gate_weights, gate_proj, up_proj, down_proj):
    tok_dev, features = tokens.shape
    top_count = expert_ids.shape[1]
    node_count = lax.axis_size("node")
    local_count = lax.axis_size("local")
    experts = EPG * node_count
    wsplit = local_count // EPG
    capacity = 4 * tok_dev * top_count // (3 * experts)
    devices = node_count * local_count
    slots = devices * capacity
    axes = ("node", "local")

    matches = expert_ids[:, :, None] == jnp.arange(experts, dtype=jnp.int32)[None, None, :]
    chosen = jnp.sum(matches.astype(jnp.int32), axis=1)
    weight = jnp.sum(jnp.where(matches, gate_weights[:, :, None], 0.0), axis=1)
    ranking = jnp.cumsum(chosen, axis=0) - chosen
    slot_ids = jnp.arange(capacity, dtype=jnp.int32)
    selected = (chosen.T[:, None, :] == 1) & (ranking.T[:, None, :] == slot_ids[None, :, None])
    pick = jnp.broadcast_to(selected[:, None], (experts, wsplit, capacity, tok_dev))
    pick = pick.reshape(slots, tok_dev)
    scale = jnp.broadcast_to(
        jnp.where(selected, weight.T[:, None, :], 0.0)[:, None], (experts, wsplit, capacity, tok_dev)
    ).reshape(slots, tok_dev)
    scale_high = scale.astype(jnp.bfloat16)
    scale_low = (scale - scale_high.astype(jnp.float32)).astype(jnp.bfloat16)

    gate_mat, up_mat, down_mat = gate_proj[0], up_proj[0], down_proj[0]
    pick = pick.astype(jnp.bfloat16)

    step = features // IN_CHUNKS
    gate_act = up_act = None
    for part in range(IN_CHUNKS):
        cols = slice(part * step, (part + 1) * step)
        packed = jnp.dot(pick, tokens[:, cols], preferred_element_type=jnp.float32).astype(jnp.bfloat16)
        rows = lax.all_to_all(
            packed.reshape(devices, capacity, step), axes, split_axis=0, concat_axis=0, tiled=True
        ).reshape(slots, step)
        gate_part = jnp.dot(rows, gate_mat[cols], preferred_element_type=jnp.float32)
        up_part = jnp.dot(rows, up_mat[cols], preferred_element_type=jnp.float32)
        gate_act = gate_part if part == 0 else gate_act + gate_part
        up_act = up_part if part == 0 else up_act + up_part
    hidden = (jax.nn.silu(gate_act) * up_act).astype(jnp.bfloat16)

    step = features // OUT_CHUNKS
    pieces = []
    for part in range(OUT_CHUNKS):
        cols = slice(part * step, (part + 1) * step)
        output = jnp.dot(hidden, down_mat[:, cols], preferred_element_type=jnp.float32).astype(jnp.bfloat16)
        returned = lax.all_to_all(
            output.reshape(devices, capacity, step), axes, split_axis=0, concat_axis=0, tiled=True
        ).reshape(slots, step)
        contract = (((0,), (0,)), ((), ()))
        total = lax.dot_general(scale_high, returned, contract, preferred_element_type=jnp.float32)
        total += lax.dot_general(scale_low, returned, contract, preferred_element_type=jnp.float32)
        pieces.append(total.astype(jnp.bfloat16))
    return pieces[0] if OUT_CHUNKS == 1 else jnp.concatenate(pieces, axis=1)


def solution(mesh):
    row = P(("parts", "node", "local"), None)
    mat = P(("node", "local"), None, None)
    return jax.shard_map(
        on_device,
        mesh=mesh,
        in_specs=(row, row, row, mat, mat, mat),
        out_specs=row,
        check_vma=False,
    )
```

```python
import jax
import jax.numpy as jnp
from jax import lax
from jax.experimental import pallas as pl
from jax.experimental.pallas import tpu as pltpu
from jax.sharding import PartitionSpec as P


EPG = 4
AXES = ("node", "local")


def dot(a, b):
    return jnp.dot(a, b, preferred_element_type=jnp.float32)


def routing(expert_ids, gate_weights, shards, wsplit, capacity):
    matches = expert_ids[None] == (shards // wsplit)[:, None, None]
    chosen = jnp.sum(matches.astype(jnp.int32), axis=1)
    weight = jnp.sum(jnp.where(matches, gate_weights[None], 0.0), axis=1)
    ranking = jnp.cumsum(chosen, axis=1) - chosen
    slot_ids = jnp.arange(capacity, dtype=jnp.int32)
    selected = (chosen[:, None, :] == 1) & (ranking[:, None, :] == slot_ids[None, :, None])
    scale = jnp.where(selected, weight[:, None, :], 0.0)
    slots = shards.shape[0] * capacity
    high = lax.reduce_precision(scale, exponent_bits=8, mantissa_bits=7)
    low = (scale - high).astype(jnp.bfloat16)
    flat = lambda a: a.reshape(slots, -1)
    return flat(selected.astype(jnp.bfloat16)), flat(high.astype(jnp.bfloat16)), flat(low)


def weighted_rows(high, low, rows):
    contract = (((0,), (0,)), ((), ()))
    total = lax.dot_general(high, rows, contract, preferred_element_type=jnp.float32)
    return total + lax.dot_general(low, rows, contract, preferred_element_type=jnp.float32)


VMEM_WHOLE = pl.BlockSpec(memory_space=pltpu.VMEM)
HBM_WHOLE = pl.BlockSpec(memory_space=pl.ANY)
UP_GROUPS, DOWN_GROUPS, LANES = 4, 2, 512


def groups_of(size, count):
    tiles = size // 128
    count = min(count, tiles)
    edges = [tiles * i // count * 128 for i in range(count + 1)]
    return [pl.ds(a, b - a) for a, b in zip(edges, edges[1:])]


def ffn_kernel(rows_ref, gate_hbm, up_hbm, down_hbm, out_ref, *scratch):
    gate_buf, up_buf, down_buf, gate_sum, up_sum, hidden_ref, gate_sem, up_sem, down_sem = scratch
    depth, width = gate_buf.shape
    up_groups, down_groups = groups_of(depth, UP_GROUPS), groups_of(depth, DOWN_GROUPS)
    gates = [pltpu.make_async_copy(gate_hbm.at[g], gate_buf.at[g], gate_sem.at[i]) for i, g in enumerate(up_groups)]
    ups = [pltpu.make_async_copy(up_hbm.at[g], up_buf.at[g], up_sem.at[i]) for i, g in enumerate(up_groups)]
    downs = [
        pltpu.make_async_copy(down_hbm.at[:, g], down_buf.at[:, g], down_sem.at[i])
        for i, g in enumerate(down_groups)
    ]
    for gate, up in zip(gates, ups):
        gate.start()
        up.start()
    for down in downs:
        down.start()
    tiles = [pl.ds(at, min(LANES, width)) for at in range(0, width, LANES)]
    for i, (group, gate, up) in enumerate(zip(up_groups, gates, ups)):
        for copy, buf, total in ((gate, gate_buf, gate_sum), (up, up_buf, up_sum)):
            copy.wait()
            for tile in tiles:
                value = dot(rows_ref[:, group], buf[group, tile])
                total[:, tile] = value if i == 0 else total[:, tile] + value
    for tile in tiles:
        hidden_ref[:, tile] = (jax.nn.silu(gate_sum[:, tile]) * up_sum[:, tile]).astype(jnp.bfloat16)
    for group, down in zip(down_groups, downs):
        down.wait()
        out_ref[:, group] = dot(hidden_ref[...], down_buf[:, group]).astype(jnp.bfloat16)


def ffn(rows, gate_mat, up_mat, down_mat):
    count, features = rows.shape
    width = gate_mat.shape[1]
    return pl.pallas_call(
        ffn_kernel,
        in_specs=[VMEM_WHOLE] + [HBM_WHOLE] * 3,
        out_specs=VMEM_WHOLE,
        out_shape=jax.ShapeDtypeStruct((count, features), jnp.bfloat16),
        scratch_shapes=[pltpu.VMEM(mat.shape, jnp.bfloat16) for mat in (gate_mat, up_mat, down_mat)]
        + [pltpu.VMEM((count, width), kind) for kind in (jnp.float32, jnp.float32, jnp.bfloat16)]
        + [pltpu.SemaphoreType.DMA((n,)) for n in (UP_GROUPS, UP_GROUPS, DOWN_GROUPS)],
        compiler_params=pltpu.CompilerParams(vmem_limit_bytes=48 << 20),
        cost_estimate=pl.CostEstimate(
            flops=6 * count * width * features,
            bytes_accessed=6 * width * features + 4 * count * features,
            transcendentals=count * width,
        ),
    )(rows, gate_mat, up_mat, down_mat)


def on_device(tokens, expert_ids, gate_weights, gate_proj, up_proj, down_proj):
    tok_dev, _ = tokens.shape
    top_count = expert_ids.shape[1]
    node_count = lax.axis_size("node")
    local_count = lax.axis_size("local")
    capacity = 4 * tok_dev * top_count // (3 * EPG * node_count)
    wsplit = local_count // EPG
    half = local_count // 2
    groups = [
        [n * local_count + side * half + i for n in range(node_count) for i in range(half)]
        for side in range(2)
    ]
    members = node_count * half
    slots = members * capacity
    gate_mat, up_mat, down_mat = gate_proj[0], up_proj[0], down_proj[0]

    across = [(i, (i + half) % local_count) for i in range(local_count)]

    def cross(array):
        return lax.ppermute(array, "local", across)

    def swap(rows):
        width = rows.shape[1]
        moved = lax.all_to_all(rows.reshape(members, capacity, width), AXES, 0, 0, axis_index_groups=groups, tiled=True)
        return moved.reshape(slots, width)

    ids, weights = expert_ids.T, gate_weights.T
    table = cross(jnp.concatenate([ids.astype(jnp.float32), weights]))
    far_tokens = cross(tokens)
    member = jnp.arange(members, dtype=jnp.int32)
    first = lax.axis_index("local") // half * half
    shards = member // half * local_count + first + member % half

    pick, high, low = routing(ids, weights, shards, wsplit, capacity)
    rows = swap(dot(pick, tokens).astype(jnp.bfloat16))
    rows, table, far_tokens = lax.optimization_barrier((rows, table, far_tokens))
    far_pick, far_high, far_low = routing(
        table[:top_count].astype(jnp.int32), table[top_count:], shards, wsplit, capacity
    )
    far_tokens, far_pick, far_high, far_low, high, low = lax.optimization_barrier(
        (far_tokens, far_pick, far_high, far_low, high, low)
    )
    far_rows = swap(dot(far_pick, far_tokens).astype(jnp.bfloat16))
    output = ffn(rows, gate_mat, up_mat, down_mat)
    far_output = ffn(far_rows, gate_mat, up_mat, down_mat)
    far_returned = swap(far_output)
    arrived = cross(weighted_rows(far_high, far_low, far_returned).astype(jnp.bfloat16))
    returned = swap(output)
    return (weighted_rows(high, low, returned) + arrived.astype(jnp.float32)).astype(jnp.bfloat16)


def solution(mesh):
    row = P(("parts", "node", "local"), None)
    mat = P(("node", "local"), None, None)

    return jax.shard_map(
        on_device,
        mesh=mesh,
        in_specs=(row, row, row, mat, mat, mat),
        out_specs=row,
        check_vma=False,
    )
```

```python
import jax
import jax.numpy as jnp
from jax import lax
from jax.experimental import pallas as pl
from jax.experimental.pallas import tpu as pltpu
from jax.sharding import PartitionSpec as P


EPG = 4
AXES = ("node", "local")


def dot(a, b):
    return jnp.dot(a, b, preferred_element_type=jnp.float32)


def routing(expert_ids, gate_weights, shards, wsplit, capacity):
    matches = expert_ids[None] == (shards // wsplit)[:, None, None]
    chosen = jnp.sum(matches.astype(jnp.int32), axis=1)
    weight = jnp.sum(jnp.where(matches, gate_weights[None], 0.0), axis=1)
    ranking = jnp.cumsum(chosen, axis=1) - chosen
    slot_ids = jnp.arange(capacity, dtype=jnp.int32)
    selected = (chosen[:, None, :] == 1) & (ranking[:, None, :] == slot_ids[None, :, None])
    scale = jnp.where(selected, weight[:, None, :], 0.0)
    slots = shards.shape[0] * capacity
    high = lax.reduce_precision(scale, exponent_bits=8, mantissa_bits=7)
    low = (scale - high).astype(jnp.bfloat16)
    flat = lambda a: a.reshape(slots, -1)
    return flat(selected.astype(jnp.bfloat16)), flat(high.astype(jnp.bfloat16)), flat(low)


def weighted_rows(high, low, rows):
    contract = (((0,), (0,)), ((), ()))
    total = lax.dot_general(high, rows, contract, preferred_element_type=jnp.float32)
    return total + lax.dot_general(low, rows, contract, preferred_element_type=jnp.float32)


VMEM_WHOLE = pl.BlockSpec(memory_space=pltpu.VMEM)
HBM_WHOLE = pl.BlockSpec(memory_space=pl.ANY)
UP_GROUPS, DOWN_GROUPS, LANES = 7, 2, 512


def groups_of(size, count):
    tiles = size // 128
    count = min(count, tiles)
    edges = [tiles * i // count * 128 for i in range(count + 1)]
    return [pl.ds(a, b - a) for a, b in zip(edges, edges[1:])]


def ffn_kernel(rows_ref, gate_hbm, up_hbm, down_hbm, out_ref, *scratch):
    gate_buf, up_buf, down_buf, gate_sum, up_sum, hidden_ref, gate_sem, up_sem, down_sem = scratch
    depth, width = gate_buf.shape
    up_groups, down_groups = groups_of(depth, UP_GROUPS), groups_of(depth, DOWN_GROUPS)
    gates = [pltpu.make_async_copy(gate_hbm.at[g], gate_buf.at[g], gate_sem.at[i]) for i, g in enumerate(up_groups)]
    ups = [pltpu.make_async_copy(up_hbm.at[g], up_buf.at[g], up_sem.at[i]) for i, g in enumerate(up_groups)]
    downs = [
        pltpu.make_async_copy(down_hbm.at[:, g], down_buf.at[:, g], down_sem.at[i])
        for i, g in enumerate(down_groups)
    ]
    for gate, up in zip(gates, ups):
        gate.start()
        up.start()
    for down in downs:
        down.start()
    tiles = [pl.ds(at, min(LANES, width)) for at in range(0, width, LANES)]
    for i, (group, gate, up) in enumerate(zip(up_groups, gates, ups)):
        for copy, buf, total in ((gate, gate_buf, gate_sum), (up, up_buf, up_sum)):
            copy.wait()
            for tile in tiles:
                value = dot(rows_ref[:, group], buf[group, tile])
                total[:, tile] = value if i == 0 else total[:, tile] + value
    for tile in tiles:
        hidden_ref[:, tile] = (jax.nn.silu(gate_sum[:, tile]) * up_sum[:, tile]).astype(jnp.bfloat16)
    for group, down in zip(down_groups, downs):
        down.wait()
        out_ref[:, group] = dot(hidden_ref[...], down_buf[:, group]).astype(jnp.bfloat16)


def ffn(rows, gate_mat, up_mat, down_mat):
    count, features = rows.shape
    width = gate_mat.shape[1]
    return pl.pallas_call(
        ffn_kernel,
        in_specs=[VMEM_WHOLE] + [HBM_WHOLE] * 3,
        out_specs=VMEM_WHOLE,
        out_shape=jax.ShapeDtypeStruct((count, features), jnp.bfloat16),
        scratch_shapes=[pltpu.VMEM(mat.shape, jnp.bfloat16) for mat in (gate_mat, up_mat, down_mat)]
        + [pltpu.VMEM((count, width), kind) for kind in (jnp.float32, jnp.float32, jnp.bfloat16)]
        + [pltpu.SemaphoreType.DMA((n,)) for n in (UP_GROUPS, UP_GROUPS, DOWN_GROUPS)],
        compiler_params=pltpu.CompilerParams(vmem_limit_bytes=48 << 20),
        cost_estimate=pl.CostEstimate(
            flops=6 * count * width * features,
            bytes_accessed=6 * width * features + 4 * count * features,
            transcendentals=count * width,
        ),
    )(rows, gate_mat, up_mat, down_mat)


def on_device(tokens, expert_ids, gate_weights, gate_proj, up_proj, down_proj):
    tok_dev, _ = tokens.shape
    top_count = expert_ids.shape[1]
    node_count = lax.axis_size("node")
    local_count = lax.axis_size("local")
    capacity = 4 * tok_dev * top_count // (3 * EPG * node_count)
    wsplit = local_count // EPG
    half = local_count // 2
    groups = [
        [n * local_count + side * half + i for n in range(node_count) for i in range(half)]
        for side in range(2)
    ]
    members = node_count * half
    slots = members * capacity
    gate_mat, up_mat, down_mat = gate_proj[0], up_proj[0], down_proj[0]

    across = [(i, (i + half) % local_count) for i in range(local_count)]

    def cross(array):
        return lax.ppermute(array, "local", across)

    def swap(rows):
        width = rows.shape[1]
        moved = lax.all_to_all(rows.reshape(members, capacity, width), AXES, 0, 0, axis_index_groups=groups, tiled=True)
        return moved.reshape(slots, width)

    ids, weights = expert_ids.T, gate_weights.T
    table = cross(jnp.concatenate([ids.astype(jnp.float32), weights]))
    far_tokens = cross(tokens)
    member = jnp.arange(members, dtype=jnp.int32)
    first = lax.axis_index("local") // half * half
    shards = member // half * local_count + first + member % half

    pick, high, low = routing(ids, weights, shards, wsplit, capacity)
    packed = dot(pick, tokens).astype(jnp.bfloat16)
    rows = swap(packed)
    far_tokens, table, _ = lax.optimization_barrier((far_tokens, table, packed))
    far_pick, far_high, far_low = routing(
        table[:top_count].astype(jnp.int32), table[top_count:], shards, wsplit, capacity
    )
    far_tokens, far_pick, far_high, far_low, high, low = lax.optimization_barrier(
        (far_tokens, far_pick, far_high, far_low, high, low)
    )
    far_rows = swap(dot(far_pick, far_tokens).astype(jnp.bfloat16))
    output = ffn(rows, gate_mat, up_mat, down_mat)
    far_output = ffn(far_rows, gate_mat, up_mat, down_mat)
    far_returned = swap(far_output)
    arrived = cross(weighted_rows(far_high, far_low, far_returned).astype(jnp.bfloat16))
    returned = swap(output)
    return (weighted_rows(high, low, returned) + arrived.astype(jnp.float32)).astype(jnp.bfloat16)


def solution(mesh):
    row = P(("parts", "node", "local"), None)
    mat = P(("node", "local"), None, None)

    return jax.shard_map(
        on_device,
        mesh=mesh,
        in_specs=(row, row, row, mat, mat, mat),
        out_specs=row,
        check_vma=False,
    )
```

```python
import jax
import jax.numpy as jnp
from jax import lax
from jax.experimental import pallas as pl
from jax.experimental.pallas import tpu as pltpu
from jax.sharding import PartitionSpec as P


EPG = 4
AXES = ("node", "local")


def dot(a, b):
    return jnp.dot(a, b, preferred_element_type=jnp.float32)


def routing(expert_ids, gate_weights, shards, wsplit, capacity):
    matches = expert_ids[None] == (shards // wsplit)[:, None, None]
    chosen = jnp.sum(matches.astype(jnp.int32), axis=1)
    weight = jnp.sum(jnp.where(matches, gate_weights[None], 0.0), axis=1)
    ranking = jnp.cumsum(chosen, axis=1) - chosen
    slot_ids = jnp.arange(capacity, dtype=jnp.int32)
    selected = (chosen[:, None, :] == 1) & (ranking[:, None, :] == slot_ids[None, :, None])
    scale = jnp.where(selected, weight[:, None, :], 0.0)
    slots = shards.shape[0] * capacity
    high = lax.reduce_precision(scale, exponent_bits=8, mantissa_bits=7)
    low = (scale - high).astype(jnp.bfloat16)
    flat = lambda a: a.reshape(slots, -1)
    return flat(selected.astype(jnp.bfloat16)), flat(high.astype(jnp.bfloat16)), flat(low)


def weighted_rows(high, low, rows):
    contract = (((0,), (0,)), ((), ()))
    total = lax.dot_general(high, rows, contract, preferred_element_type=jnp.float32)
    return total + lax.dot_general(low, rows, contract, preferred_element_type=jnp.float32)


VMEM_WHOLE = pl.BlockSpec(memory_space=pltpu.VMEM)
HBM_WHOLE = pl.BlockSpec(memory_space=pl.ANY)
UP_GROUPS, DOWN_GROUPS, LANES = 7, 1, 512


def groups_of(size, count):
    tiles = size // 128
    count = min(count, tiles)
    edges = [tiles * i // count * 128 for i in range(count + 1)]
    return [pl.ds(a, b - a) for a, b in zip(edges, edges[1:])]


def ffn_kernel(rows_ref, gate_hbm, up_hbm, down_hbm, out_ref, *scratch):
    gate_buf, up_buf, down_buf, gate_sum, up_sum, hidden_ref, gate_sem, up_sem, down_sem = scratch
    depth, width = gate_buf.shape
    up_groups, down_groups = groups_of(depth, UP_GROUPS), groups_of(depth, DOWN_GROUPS)
    gates = [pltpu.make_async_copy(gate_hbm.at[g], gate_buf.at[g], gate_sem.at[i]) for i, g in enumerate(up_groups)]
    ups = [pltpu.make_async_copy(up_hbm.at[g], up_buf.at[g], up_sem.at[i]) for i, g in enumerate(up_groups)]
    downs = [
        pltpu.make_async_copy(down_hbm.at[:, g], down_buf.at[:, g], down_sem.at[i])
        for i, g in enumerate(down_groups)
    ]
    for gate, up in zip(gates, ups):
        gate.start()
        up.start()
    for down in downs:
        down.start()
    tiles = [pl.ds(at, min(LANES, width)) for at in range(0, width, LANES)]
    for i, (group, gate, up) in enumerate(zip(up_groups, gates, ups)):
        for copy, buf, total in ((gate, gate_buf, gate_sum), (up, up_buf, up_sum)):
            copy.wait()
            for tile in tiles:
                value = dot(rows_ref[:, group], buf[group, tile])
                total[:, tile] = value if i == 0 else total[:, tile] + value
    for tile in tiles:
        hidden_ref[:, tile] = (jax.nn.silu(gate_sum[:, tile]) * up_sum[:, tile]).astype(jnp.bfloat16)
    for group, down in zip(down_groups, downs):
        down.wait()
        out_ref[:, group] = dot(hidden_ref[...], down_buf[:, group]).astype(jnp.bfloat16)


def ffn(rows, gate_mat, up_mat, down_mat):
    count, features = rows.shape
    width = gate_mat.shape[1]
    return pl.pallas_call(
        ffn_kernel,
        in_specs=[VMEM_WHOLE] + [HBM_WHOLE] * 3,
        out_specs=VMEM_WHOLE,
        out_shape=jax.ShapeDtypeStruct((count, features), jnp.bfloat16),
        scratch_shapes=[pltpu.VMEM(mat.shape, jnp.bfloat16) for mat in (gate_mat, up_mat, down_mat)]
        + [pltpu.VMEM((count, width), kind) for kind in (jnp.float32, jnp.float32, jnp.bfloat16)]
        + [pltpu.SemaphoreType.DMA((n,)) for n in (UP_GROUPS, UP_GROUPS, DOWN_GROUPS)],
        compiler_params=pltpu.CompilerParams(vmem_limit_bytes=48 << 20),
        cost_estimate=pl.CostEstimate(
            flops=6 * count * width * features,
            bytes_accessed=6 * width * features + 4 * count * features,
            transcendentals=count * width,
        ),
    )(rows, gate_mat, up_mat, down_mat)


def on_device(tokens, expert_ids, gate_weights, gate_proj, up_proj, down_proj):
    tok_dev, _ = tokens.shape
    top_count = expert_ids.shape[1]
    node_count = lax.axis_size("node")
    local_count = lax.axis_size("local")
    capacity = 4 * tok_dev * top_count // (3 * EPG * node_count)
    wsplit = local_count // EPG
    half = local_count // 2
    groups = [
        [n * local_count + side * half + i for n in range(node_count) for i in range(half)]
        for side in range(2)
    ]
    members = node_count * half
    slots = members * capacity
    gate_mat, up_mat, down_mat = gate_proj[0], up_proj[0], down_proj[0]

    across = [(i, (i + half) % local_count) for i in range(local_count)]

    def cross(array):
        return lax.ppermute(array, "local", across)

    def swap(rows):
        width = rows.shape[1]
        moved = lax.all_to_all(rows.reshape(members, capacity, width), AXES, 0, 0, axis_index_groups=groups, tiled=True)
        return moved.reshape(slots, width)

    ids, weights = expert_ids.T, gate_weights.T
    table = cross(jnp.concatenate([expert_ids.astype(jnp.float32), gate_weights], axis=1))
    far_tokens = cross(tokens)
    member = jnp.arange(members, dtype=jnp.int32)
    first = lax.axis_index("local") // half * half
    shards = member // half * local_count + first + member % half

    pick, high, low = routing(ids, weights, shards, wsplit, capacity)
    packed = dot(pick, tokens).astype(jnp.bfloat16)
    rows = swap(packed)
    far_tokens, table, _ = lax.optimization_barrier((far_tokens, table, packed))
    far_pick, far_high, far_low = routing(
        table[:, :top_count].T.astype(jnp.int32), table[:, top_count:].T, shards, wsplit, capacity
    )
    far_tokens, far_pick, far_high, far_low, high, low = lax.optimization_barrier(
        (far_tokens, far_pick, far_high, far_low, high, low)
    )
    far_rows = swap(dot(far_pick, far_tokens).astype(jnp.bfloat16))
    output = ffn(rows, gate_mat, up_mat, down_mat)
    far_output = ffn(far_rows, gate_mat, up_mat, down_mat)
    far_returned = swap(far_output)
    arrived = cross(weighted_rows(far_high, far_low, far_returned).astype(jnp.bfloat16))
    returned = swap(output)
    return (weighted_rows(high, low, returned) + arrived.astype(jnp.float32)).astype(jnp.bfloat16)


def solution(mesh):
    row = P(("parts", "node", "local"), None)
    mat = P(("node", "local"), None, None)

    return jax.shard_map(
        on_device,
        mesh=mesh,
        in_specs=(row, row, row, mat, mat, mat),
        out_specs=row,
        check_vma=False,
    )
```
